32 devices in a mesh: seq: 8 (over z, x), hx: 4 (over y, core).
Axes of the slice: x: 2, y: 2, z: 4, core: 2. Of those that a mesh axis runs over, the one named last changes fastest.
Arguments:
- query: bfloat16 [8192, 8192], P('seq', 'hx'), may hold values from -6 to 6
- key_in: bfloat16 [8192, 8192], P('seq', 'hx'), may hold values from -6 to 6
- value: bfloat16 [8192, 8192], P('seq', 'hx'), may hold values from -6 to 6
- head_gain: float32 [8192], P('hx'), may hold values from 0.1 to 1.9
- out_weight: bfloat16 [8192, 6144], P('hx', 'seq'), may hold values from -0.0625 to 0.0625
- residual: bfloat16 [8192, 6144], P(('seq', 'hx')), may hold values from -6 to 6
Outputs:
- mixed: bfloat16 [8192, 6144], P(('seq', 'hx'))
The draws below stay inside these ranges and needn't reach their ends.
All inputs are finite; a program needn't handle non-finite values.
Results may differ from the reference program's by a relative error of at most 0.014.
Values may be sent and summed in bfloat16 or wider, within the bound.
A program may use at most 128 MiB of HBM per device.

```python
import jax
import jax.numpy as jnp
from jax import lax

D = 6144
HEADS = 64
DH = 128
TOK_DEV = 1024
TOKENS = 8192
HEAD_GROUPS = 4


def levels(stream_key, shape, split, low, high):
    loudness, own = 1.0, jax.random.fold_in(stream_key, 6)
    for position, shards_of in split:
        steps = jnp.exp(jax.random.uniform(jax.random.fold_in(own, position), (shards_of,), jnp.float32, low / len(split), high / len(split)))
        loudness = loudness * jnp.repeat(steps, shape[position] // shards_of).reshape([-1 if axis == position else 1 for axis in range(len(shape))])
    return loudness


def bell_draw(stream_key, extent, scale, reach, shards=(), kind=jnp.bfloat16):
    gain = levels(stream_key, extent, shards, -0.22, 0.18) if shards else 1.0
    entries = jax.random.normal(stream_key, extent, jnp.float32) * scale * gain
    return jnp.minimum(jnp.maximum(entries, -reach), reach).astype(kind)


def setup_inputs(seed: int = 0) -> dict:
    keys = jax.random.split(jax.random.key(seed), 7)
    return {
        "query": bell_draw(keys[0], (TOKENS, HEADS * DH), 1.0, 6.0, ((0, 8), (1, 4))),
        "key_in": bell_draw(keys[1], (TOKENS, HEADS * DH), 1.0, 6.0, ((0, 8), (1, 4))),
        "value": bell_draw(keys[2], (TOKENS, HEADS * DH), 1.0, 6.0, ((0, 8), (1, 4))),
        "head_gain": jnp.clip(1.0 + 0.18 * jax.random.normal(keys[3], (HEADS * DH,), jnp.float32), 0.1, 1.9),
        "out_weight": bell_draw(keys[4], (HEADS * DH, D), (HEADS * DH) ** -0.5, 0.0625, ((0, 4), (1, 8))),
        "residual": bell_draw(keys[5], (TOKENS, D), 1.0, 6.0, ((0, 32),)),
    }


def activate(array):
    return jax.nn.silu(array.astype(jnp.float32)).astype(jnp.bfloat16)

def reference(query, key_in, value, head_gain, out_weight, residual):
    q_act = activate(query)
    k_act = activate(key_in)
    blocks = min(512, TOK_DEV)
    count = TOKENS // blocks
    q_blocks = q_act.reshape(count, blocks, HEADS, DH)
    k_blocks = k_act.reshape(count, blocks, HEADS, DH)
    v_blocks = value.reshape(count, blocks, HEADS, DH)
    rows = jnp.arange(blocks, dtype=jnp.int32)
    lower = rows[:, None] >= rows[None, :]
    highest = lax.Precision.HIGHEST

    def advance(state, inputs):
        q_part, k_part, v_part = inputs
        q_full = q_part.astype(jnp.float32)
        k_full = k_part.astype(jnp.float32)
        v_full = v_part.astype(jnp.float32)
        scores = jnp.einsum('thd,shd->hts', q_full, k_full, precision=highest)
        scores = jnp.where(lower[None, :, :], scores, jnp.zeros_like(scores))
        inner = jnp.einsum('hts,she->the', scores, v_full, precision=highest)
        outer = jnp.einsum('thd,hde->the', q_full, state, precision=highest)
        state = state + jnp.einsum('thd,the->hde', k_full, v_full, precision=highest)
        return (state, inner + outer)
    start = jnp.zeros((HEADS, DH, DH), jnp.float32)
    unused, attended = lax.scan(advance, start, (q_blocks, k_blocks, v_blocks))
    attended = attended.reshape(TOKENS, HEADS, DH)
    meansq = lax.optimization_barrier(jnp.mean(attended * attended, axis=-1, keepdims=True))
    normed = attended * lax.rsqrt(meansq + 1e-06) * head_gain.reshape(HEADS, DH)
    normed = normed.astype(jnp.bfloat16).reshape(TOKENS, HEADS * DH)
    group_width = HEADS * DH // HEAD_GROUPS
    total = residual.astype(jnp.float32)
    for group in range(HEAD_GROUPS):
        lo_col = group * group_width
        part = jnp.dot(normed[:, lo_col:lo_col + group_width], out_weight[lo_col:lo_col + group_width, :], preferred_element_type=jnp.float32)
        part = lax.optimization_barrier(part.astype(jnp.bfloat16))
        total = total + part.astype(jnp.float32)
    return total.astype(jnp.bfloat16)
```

```python
import functools

import jax
import jax.numpy as jnp
import numpy as np
from jax import lax
from jax.experimental import pallas as pl
from jax.experimental.pallas import tpu as pltpu
from jax.sharding import PartitionSpec as P

DH = 128
CORES = 2


def pick(table, index):
    return lax.dynamic_index_in_dim(jnp.asarray(table), index, 0, keepdims=False, allow_negative_indices=False)


def silu(x):
    x = x.astype(jnp.float32)
    return (x / (1.0 + jnp.exp(-x))).astype(jnp.bfloat16)


def state_kernel(k_ref, v_ref, out_ref):
    both = lax.dot_general(
        silu(k_ref[...]), v_ref[...], (((0,), (0,)), ((), ())),
        preferred_element_type=jnp.float32,
    )
    for i in range(out_ref.shape[0]):
        out_ref[i] = both[i * DH : (i + 1) * DH, i * DH : (i + 1) * DH].astype(out_ref.dtype)


def attend_kernel(chunks, place_ref, q_ref, k_ref, v_ref, state_ref, gain_ref, out_ref):
    rows = q_ref.shape[0] // chunks
    lower = lax.broadcasted_iota(jnp.int32, (rows, rows), 0) >= lax.broadcasted_iota(
        jnp.int32, (rows, rows), 1
    )
    for i in range(state_ref.shape[0]):
        cols = slice(i * DH, (i + 1) * DH)
        state = state_ref[i]
        gain = gain_ref[:, cols]
        for c in range(chunks):
            span = slice(c * rows, (c + 1) * rows)
            q, k, v = silu(q_ref[span, cols]), silu(k_ref[span, cols]), v_ref[span, cols]
            scores = lax.dot_general(
                q, k, (((1,), (1,)), ((), ())), preferred_element_type=jnp.float32
            )
            scores = jnp.where(lower, scores, 0.0).astype(jnp.bfloat16)
            att = jnp.dot(scores, v, preferred_element_type=jnp.float32)
            att += jnp.dot(q, state.astype(jnp.bfloat16), preferred_element_type=jnp.float32)
            if c + 1 < chunks:
                state = state + lax.dot_general(
                    k, v, (((0,), (0,)), ((), ())), preferred_element_type=jnp.float32
                )
            meansq = jnp.mean(att * att, axis=-1, keepdims=True)
            normed = att * lax.rsqrt(meansq + 1e-06) * gain
            start = pl.multiple_of(place_ref[c] * rows, rows)
            out_ref[pl.ds(start, rows), cols] = normed.astype(out_ref.dtype)


def local_states(key_in, value, pair):
    tokens, width = key_in.shape
    heads = width // DH
    block = pl.BlockSpec((tokens, pair * DH), lambda h: (0, h))
    return pl.pallas_call(
        state_kernel,
        grid=(heads // pair,),
        in_specs=[block, block],
        out_specs=pl.BlockSpec((pair, DH, DH), lambda h: (h, 0, 0)),
        out_shape=jax.ShapeDtypeStruct((heads, DH, DH), jnp.float32),
        cost_estimate=pl.CostEstimate(
            flops=4 * tokens * width * DH, bytes_accessed=4 * tokens * width, transcendentals=tokens * width
        ),
        name="states",
    )(key_in, value)


def attend(place, query, key_in, value, prefix, head_gain, chunks, pair):
    tokens, width = query.shape
    heads = width // DH
    block = pl.BlockSpec((tokens, pair * DH), lambda h, place: (0, h))
    return pl.pallas_call(
        functools.partial(attend_kernel, chunks),
        grid_spec=pltpu.PrefetchScalarGridSpec(
            num_scalar_prefetch=1,
            grid=(heads // pair,),
            in_specs=[
                block, block, block,
                pl.BlockSpec((pair, DH, DH), lambda h, place: (h, 0, 0)),
                pl.BlockSpec((1, pair * DH), lambda h, place: (0, h)),
            ],
            out_specs=block,
        ),
        out_shape=jax.ShapeDtypeStruct((tokens, width), jnp.bfloat16),
        cost_estimate=pl.CostEstimate(
            flops=8 * tokens * width * DH, bytes_accessed=8 * tokens * width, transcendentals=2 * tokens * width
        ),
        name="attend",
    )(place, query, key_in, value, prefix, head_gain.reshape(1, width))


def prefix_of(states, n):
    me = lax.axis_index("seq")
    sent = states.astype(jnp.bfloat16)
    other = lax.ppermute(sent, "seq", [(i, i ^ 1) for i in range(n)]).astype(jnp.float32)
    total = other + sent.astype(jnp.float32)
    prefix = jnp.where(me % 2 == 1, other, 0.0)
    step, reach = 2, total
    while step < n:
        got = lax.ppermute(
            reach.astype(jnp.bfloat16), "seq", [(i, i + step) for i in range(n - step)]
        ).astype(jnp.float32)
        prefix, reach = prefix + got, reach + got
        step *= 2
    return prefix


def per_device(seq, hx, query, key_in, value, head_gain, out_weight, residual):
    tokens, width = query.shape
    shard = out_weight.shape[1]
    half = shard // 2
    rows = tokens // hx
    groups = hx // CORES
    me = lax.axis_index("seq")

    ring = list(range(0, seq, 2)) + list(range(seq - 1, 0, -2))
    spot = [ring.index(i) for i in range(seq)]
    ahead = [(ring[i], ring[(i + 1) % seq]) for i in range(seq)]
    back = [(b, a) for a, b in ahead]

    distances = [0]
    for step in range(1, (seq - 1) // 2 + 1):
        distances += [seq - step, step]
    distances.append(seq // 2)
    table = np.array([[ring[(spot[i] + d) % seq] * shard for d in distances] for i in range(seq)], np.int32)
    row = pick(table, me)
    columns = [pick(row, i) for i in range(len(distances))]
    columns.append(columns[-1] + half)

    weights = [out_weight]
    right = left = out_weight
    for step in range(1, (seq - 1) // 2 + 1):
        right = lax.ppermute(right, "seq", ahead)
        left = lax.ppermute(left, "seq", back)
        weights += [right, left]
    weights.append(lax.ppermute(right[:, :half], "seq", ahead))
    weights.append(lax.ppermute(left[:, half:], "seq", back))

    pair = 2
    prefix = prefix_of(local_states(key_in, value, pair), seq)
    place = pick(
        np.array(
            [
                [(b // CORES - d // CORES) % groups + groups * (b % CORES == d % CORES) for b in range(hx)]
                for d in range(hx)
            ],
            np.int32,
        ),
        lax.axis_index("hx"),
    )
    normed = attend(place, query, key_in, value, prefix, head_gain, hx, pair)
    theirs, ours = normed[: tokens // 2], normed[tokens // 2 :]

    swap = [(i, i ^ 1) for i in range(hx)]
    out = residual
    for weight, column in zip(weights, columns):
        got = lax.ppermute(
            jnp.dot(theirs, weight, preferred_element_type=jnp.float32).astype(jnp.bfloat16), "hx", swap
        )
        total = jnp.dot(ours, weight, preferred_element_type=jnp.float32) + got.astype(jnp.float32)
        mixed = total[:rows]
        for j in range(1, groups):
            mixed = mixed + lax.ppermute(
                total[j * rows : (j + 1) * rows].astype(jnp.bfloat16),
                "hx",
                [(i, (i // CORES + j) % groups * CORES + i % CORES) for i in range(hx)],
            ).astype(jnp.float32)
        kept = lax.dynamic_slice(residual, (0, column), mixed.shape, allow_negative_indices=False).astype(jnp.float32)
        out = lax.dynamic_update_slice(
            out, (mixed + kept).astype(jnp.bfloat16), (0, column), allow_negative_indices=False
        )
    return out


def solution(mesh):
    seq, hx = mesh.shape["seq"], mesh.shape["hx"]
    return jax.shard_map(
        functools.partial(per_device, seq, hx),
        mesh=mesh,
        in_specs=(
            P("seq", "hx"),
            P("seq", "hx"),
            P("seq", "hx"),
            P("hx"),
            P("hx", "seq"),
            P(("seq", "hx"), None),
        ),
        out_specs=P(("seq", "hx"), None),
        check_vma=False,
    )
```

```python
import functools

import jax
import jax.numpy as jnp
import numpy as np
from jax import lax
from jax.experimental import pallas as pl
from jax.experimental.pallas import tpu as pltpu
from jax.sharding import PartitionSpec as P

DH = 128
CORES = 2


def pick(table, index):
    return lax.dynamic_index_in_dim(jnp.asarray(table), index, 0, keepdims=False, allow_negative_indices=False)


def silu(x):
    x = x.astype(jnp.float32)
    return (x / (1.0 + jnp.exp(-x))).astype(jnp.bfloat16)


def state_kernel(k_ref, v_ref, out_ref):
    both = lax.dot_general(
        silu(k_ref[...]), v_ref[...], (((0,), (0,)), ((), ())),
        preferred_element_type=jnp.float32,
    )
    for i in range(out_ref.shape[0]):
        out_ref[i] = both[i * DH : (i + 1) * DH, i * DH : (i + 1) * DH].astype(out_ref.dtype)


def attend_kernel(chunks, place_ref, q_ref, k_ref, v_ref, state_ref, gain_ref, out_ref):
    rows = q_ref.shape[0] // chunks
    lower = lax.broadcasted_iota(jnp.int32, (rows, rows), 0) >= lax.broadcasted_iota(
        jnp.int32, (rows, rows), 1
    )
    for i in range(state_ref.shape[0]):
        cols = slice(i * DH, (i + 1) * DH)
        state = state_ref[i]
        gain = gain_ref[:, cols]
        for c in range(chunks):
            span = slice(c * rows, (c + 1) * rows)
            q, k, v = silu(q_ref[span, cols]), silu(k_ref[span, cols]), v_ref[span, cols]
            scores = lax.dot_general(
                q, k, (((1,), (1,)), ((), ())), preferred_element_type=jnp.float32
            )
            scores = jnp.where(lower, scores, 0.0).astype(jnp.bfloat16)
            att = jnp.dot(scores, v, preferred_element_type=jnp.float32)
            att += jnp.dot(q, state.astype(jnp.bfloat16), preferred_element_type=jnp.float32)
            if c + 1 < chunks:
                state = state + lax.dot_general(
                    k, v, (((0,), (0,)), ((), ())), preferred_element_type=jnp.float32
                )
            meansq = jnp.mean(att * att, axis=-1, keepdims=True)
            normed = att * lax.rsqrt(meansq + 1e-06) * gain
            start = pl.multiple_of(place_ref[c] * rows, rows)
            out_ref[pl.ds(start, rows), cols] = normed.astype(out_ref.dtype)


def local_states(key_in, value, pair):
    tokens, width = key_in.shape
    heads = width // DH
    block = pl.BlockSpec((tokens, pair * DH), lambda h: (0, h))
    return pl.pallas_call(
        state_kernel,
        grid=(heads // pair,),
        in_specs=[block, block],
        out_specs=pl.BlockSpec((pair, DH, DH), lambda h: (h, 0, 0)),
        out_shape=jax.ShapeDtypeStruct((heads, DH, DH), jnp.float32),
        cost_estimate=pl.CostEstimate(
            flops=4 * tokens * width * DH, bytes_accessed=4 * tokens * width, transcendentals=tokens * width
        ),
        name="states",
    )(key_in, value)


def attend(place, query, key_in, value, prefix, head_gain, chunks, pair):
    tokens, width = query.shape
    heads = width // DH
    block = pl.BlockSpec((tokens, pair * DH), lambda h, place: (0, h))
    return pl.pallas_call(
        functools.partial(attend_kernel, chunks),
        grid_spec=pltpu.PrefetchScalarGridSpec(
            num_scalar_prefetch=1,
            grid=(heads // pair,),
            in_specs=[
                block, block, block,
                pl.BlockSpec((pair, DH, DH), lambda h, place: (h, 0, 0)),
                pl.BlockSpec((1, pair * DH), lambda h, place: (0, h)),
            ],
            out_specs=block,
        ),
        out_shape=jax.ShapeDtypeStruct((tokens, width), jnp.bfloat16),
        cost_estimate=pl.CostEstimate(
            flops=8 * tokens * width * DH, bytes_accessed=8 * tokens * width, transcendentals=2 * tokens * width
        ),
        name="attend",
    )(place, query, key_in, value, prefix, head_gain.reshape(1, width))


def add_kernel(columns_ref, out_in_ref, total_ref, *refs):
    mixed = out_in_ref[...].astype(jnp.float32) + total_ref[...]
    for piece in refs[:-1]:
        mixed += piece[...].astype(jnp.float32)
    refs[-1][...] = mixed.astype(refs[-1].dtype)


def add_columns(columns, index, out, total, pieces):
    rows, width = out.shape[0], total.shape[1]
    block = pl.BlockSpec((rows, width), lambda g, columns: (0, columns[index]))
    first = pl.BlockSpec((rows, width), lambda g, columns: (0, 0))
    return pl.pallas_call(
        add_kernel,
        grid_spec=pltpu.PrefetchScalarGridSpec(
            num_scalar_prefetch=1,
            grid=(1,),
            in_specs=[block, first] + [first] * len(pieces),
            out_specs=block,
        ),
        out_shape=jax.ShapeDtypeStruct(out.shape, out.dtype),
        input_output_aliases={1: 0},
        cost_estimate=pl.CostEstimate(
            flops=3 * rows * width, bytes_accessed=10 * rows * width, transcendentals=0
        ),
        name="add",
    )(columns, out, total, *pieces)


def prefix_of(states, n):
    me = lax.axis_index("seq")
    sent = states.astype(jnp.bfloat16)
    other = lax.ppermute(sent, "seq", [(i, i ^ 1) for i in range(n)]).astype(jnp.float32)
    total = other + sent.astype(jnp.float32)
    prefix = jnp.where(me % 2 == 1, other, 0.0)
    step, reach = 2, total
    while step < n:
        got = lax.ppermute(
            reach.astype(jnp.bfloat16), "seq", [(i, i + step) for i in range(n - step)]
        ).astype(jnp.float32)
        prefix, reach = prefix + got, reach + got
        step *= 2
    return prefix


def per_device(seq, hx, query, key_in, value, head_gain, out_weight, residual):
    tokens, width = query.shape
    shard = out_weight.shape[1]
    split = 2 if shard % (2 * DH) == 0 else 1
    half = shard // split
    rows = tokens // hx
    groups = hx // CORES
    me = lax.axis_index("seq")

    ring = list(range(0, seq, 2)) + list(range(seq - 1, 0, -2))
    spot = [ring.index(i) for i in range(seq)]
    ahead = [(ring[i], ring[(i + 1) % seq]) for i in range(seq)]
    back = [(b, a) for a, b in ahead]

    distances = [0]
    for step in range(1, (seq - 1) // 2 + 1):
        distances += [seq - step, step]
    distances.append(seq // 2)
    table = np.array([[ring[(spot[i] + d) % seq] for d in distances] for i in range(seq)], np.int32)
    table = np.concatenate(
        [table[:, :-1]] + [split * table[:, -1:] + i for i in range(split)], axis=1
    ).astype(np.int32)
    columns = pick(table, me)

    pair = 2
    prefix = prefix_of(local_states(key_in, value, pair), seq)
    travelling, prefix = lax.optimization_barrier((out_weight, prefix))

    hops = (seq - 1) // 2
    right, left = lax.ppermute(travelling, "seq", ahead), lax.ppermute(travelling, "seq", back)
    place = pick(
        np.array(
            [
                [(b // CORES - d // CORES) % groups + groups * (b % CORES == d % CORES) for b in range(hx)]
                for d in range(hx)
            ],
            np.int32,
        ),
        lax.axis_index("hx"),
    )
    normed = attend(place, query, key_in, value, prefix, head_gain, hx, pair)
    right, left, normed = lax.optimization_barrier((right, left, normed))
    theirs, ours = normed[: tokens // 2], normed[tokens // 2 :]

    swap = [(i, i ^ 1) for i in range(hx)]

    def project(index, weight, out):
        got = lax.ppermute(
            jnp.dot(theirs, weight, preferred_element_type=jnp.float32).astype(jnp.bfloat16), "hx", swap
        )
        total = jnp.dot(ours, weight, preferred_element_type=jnp.float32) + got.astype(jnp.float32)
        pieces = [
            lax.ppermute(
                total[j * rows : (j + 1) * rows].astype(jnp.bfloat16),
                "hx",
                [(i, (i // CORES + j) % groups * CORES + i % CORES) for i in range(hx)],
            )
            for j in range(1, groups)
        ]
        return add_columns(columns, index, out, total, pieces)

    out = project(0, out_weight, residual)
    waiting = []
    for hop in range(1, hops + 1):
        waiting += [(2 * hop - 1, right), (2 * hop, left)]
        if hop < hops:
            right, left = lax.ppermute(right, "seq", ahead), lax.ppermute(left, "seq", back)
    for index, weight in waiting[:-2]:
        out = project(index, weight, out)
    right, left, out = lax.optimization_barrier((right, left, out))
    far = [lax.ppermute(right[:, :half], "seq", ahead)]
    if split > 1:
        far.append(lax.ppermute(left[:, half:], "seq", back))
    out = project(2 * hops - 1, right, out)
    out = project(2 * hops, left, out)
    for index, weight in enumerate(far):
        out = project(2 * hops + 1 + index, weight, out)
    return out


def solution(mesh):
    seq, hx = mesh.shape["seq"], mesh.shape["hx"]
    return jax.shard_map(
        functools.partial(per_device, seq, hx),
        mesh=mesh,
        in_specs=(
            P("seq", "hx"),
            P("seq", "hx"),
            P("seq", "hx"),
            P("hx"),
            P("hx", "seq"),
            P(("seq", "hx"), None),
        ),
        out_specs=P(("seq", "hx"), None),
        check_vma=False,
    )
```
